512 devices in a mesh: vol: 8 (over y, core), surf: 64 (over x, z).
Axes of the slice: x: 4, y: 4, z: 16, core: 2. Of those that a mesh axis runs over, the one named last changes fastest.
Arguments:
- vol_coords: float32 [3, 32768], P(None, 'vol'), may hold values from 0 to 64, as said below
- surf_coords: float32 [3, 65536], P(None, 'surf'), may hold values from 0 to 64, as said below
- vol_sens: bfloat16 [96, 32768], P(None, 'vol'), may hold values from -6 to 6
- links: int32 [8, 65536], P(None, 'surf'), may hold values from -1 to 65535, as said below
Outputs:
- smooth_sens: float32 [96, 65536], P('vol', 'surf')
The draws below stay inside these ranges and needn't reach their ends.
Inputs may be any that keep to these rules, and one draw needn't show every extreme that they name: `vol_coords`: row 0 is a node's span position in patch widths, within 0 to 64; row 1 its chordwise position, within 0 to 1; row 2 its height above the surface, within 0.005 to 2. `surf_coords`: surface node i belongs to patch i // 1024; row 0 of a node of patch p lies within p to p + 1, row 1 within 0 to 1, row 2 within 0 to 0.02. `links`: each valid entry of node i names a surface node of i's patch or of one of the two patches beside it on the cycle of 64 patches (patch indices taken mod 64); slot 0 is always valid, and the valid slots of a node come before its empty ones.
All inputs are finite; a program needn't handle non-finite values.
Results may differ from the reference program's by a relative error of at most 0.0003.
Values sent between devices are 32-bit elements; how exact they have to be, the bound alone decides.
A program may use at most 64 MiB of HBM per device.

```python
import jax
import jax.numpy as jnp
from jax import lax

SDEV = 1024
LINKS = 8
SWEEPS = 4
ROWS = 96
NV = 32768
PATCHES = 64
NS = 65536


def draw_vol_coords(key, part):
    keys = jax.random.split(key, 3)
    u_span = jax.random.uniform(keys[0], (NV,), jnp.float32)
    u_chord = jax.random.uniform(keys[1], (NV,), jnp.float32)
    u_height = jax.random.uniform(keys[2], (NV,), jnp.float32)
    span = PATCHES * u_span
    height = 0.005 * jnp.power(400.0, u_height)
    return jnp.stack([span, u_chord, height]).astype(jnp.float32)


def draw_surf_coords(key, part):
    keys = jax.random.split(key, 3)
    node = jnp.arange(NS, dtype=jnp.int32)
    patch = (node // SDEV).astype(jnp.float32)
    u_span = jax.random.uniform(keys[0], (NS,), jnp.float32)
    u_chord = jax.random.uniform(keys[1], (NS,), jnp.float32)
    u_height = jax.random.uniform(keys[2], (NS,), jnp.float32)
    chord = u_chord
    return jnp.stack([patch + u_span, chord, 0.02 * u_height]).astype(jnp.float32)


def draw_vol_sens(key, part):
    keys = jax.random.split(key, 1)
    rough = jax.random.truncated_normal(keys[0], -6.0, 6.0, (ROWS, NV), jnp.float32)
    values = rough
    return values.astype(jnp.float32).astype(jnp.bfloat16)


def draw_links(key, part):
    keys = jax.random.split(key, 3)
    node = jnp.arange(NS, dtype=jnp.int32)
    patch = node // SDEV
    offset = jax.random.randint(keys[0], (LINKS, NS), -1, 2, dtype=jnp.int32)
    member = jax.random.randint(keys[1], (LINKS, NS), 0, SDEV, dtype=jnp.int32)
    target = (patch[None, :] + offset + PATCHES) % PATCHES * SDEV + member
    degree = jax.random.randint(keys[2], (NS,), 4, LINKS + 1, dtype=jnp.int32)
    slot = jnp.arange(LINKS, dtype=jnp.int32)[:, None]
    first = patch * SDEV + (node + 1) % SDEV
    target = jnp.where(slot == 0, first[None, :], target)
    return jnp.where(slot < degree[None, :], target, -1).astype(jnp.int32)


def setup_inputs(seed: int = 0) -> dict:
    key_list = jax.random.split(jax.random.key(seed), 5)
    vol_coords = draw_vol_coords(jax.random.fold_in(key_list[4], 71), 0)
    surf_coords = draw_surf_coords(jax.random.fold_in(key_list[4], 71), 0)
    vol_sens = draw_vol_sens(jax.random.fold_in(key_list[4], 71), 0)
    links = draw_links(jax.random.fold_in(key_list[4], 71), 0)
    return dict(vol_coords=vol_coords, surf_coords=surf_coords, vol_sens=vol_sens, links=links)


near_square = 0.0016
far_square = 4.0
far_weight = 0.001
smoothing = 2.0


def idw_weights(vol_block, surf_block):
    delta = vol_block[0][:, None] - surf_block[0][None, :]
    dist_sq = delta * delta
    delta = vol_block[1][:, None] - surf_block[1][None, :]
    dist_sq = dist_sq + delta * delta
    delta = vol_block[2][:, None] - surf_block[2][None, :]
    dist_sq = dist_sq + delta * delta
    near = near_square / (dist_sq + near_square)
    return near * near + (far_weight * far_square) / (dist_sq + far_square)


def relax(region, index, valid, rhs, degree):
    total = jnp.zeros(rhs.shape, jnp.float32)
    for slot in range(index.shape[0]):
        picked = jnp.take(region, index[slot], axis=1)
        total = total + jnp.where(valid[slot][None, :], picked, jnp.float32(0.0))
    return (rhs + smoothing * total) / (1.0 + smoothing * degree[None, :])


def reference(vol_coords, surf_coords, vol_sens, links):
    starts = (jnp.arange(PATCHES) * SDEV).astype(jnp.int32)

    def add_totals(carry, start):
        block = lax.dynamic_slice_in_dim(surf_coords, start, SDEV, 1)
        return carry + jnp.sum(idw_weights(vol_coords, block), axis=1), None

    totals, _ = lax.scan(add_totals, jnp.zeros((NV,), jnp.float32), starts)
    scaled = vol_sens.astype(jnp.float32) / totals[None, :]

    def project(start):
        block = lax.dynamic_slice_in_dim(surf_coords, start, SDEV, 1)
        weights = idw_weights(vol_coords, block)
        return jnp.dot(scaled, weights, precision=lax.Precision.HIGHEST, preferred_element_type=jnp.float32)

    stacked = lax.map(project, starts)
    surf_sens = jnp.transpose(stacked, (1, 0, 2)).reshape(ROWS, NS)
    valid = links >= 0
    index = jnp.maximum(links, 0).astype(jnp.int32)
    degree = jnp.sum(valid.astype(jnp.float32), axis=0)
    current = surf_sens
    for sweep in range(SWEEPS):
        current = relax(current, index, valid, surf_sens, degree)
    return current
```

```python
import functools

import jax
import jax.numpy as jnp
from jax import lax
from jax.experimental import pallas as pl
from jax.experimental.pallas import tpu as pltpu
from jax.sharding import PartitionSpec as P

SWEEPS = 4
NX, NZ, NY = 4, 16, 4
PATCHES = NX * NZ
LANES = 128
MESH = pl.DeviceIdType.MESH

near_square = 0.0016
far_square = 4.0
far_weight = 0.001
smoothing = 2.0

ROWS_W = 64
ROWS_A = 64
NT = (((1,), (1,)), ((), ()))


def split(value):
    high = value.astype(jnp.bfloat16)
    low = (value - high.astype(jnp.float32)).astype(jnp.bfloat16)
    return high, low


def kernel(
    vol_ref, surf_ref, sens_ref, links_ref, out_ref,
    surf_cols, w_high, w_low, tot, rx, zsend, zbuf, inv, scaled, prod, rs, pr, ysend, yr,
    cur, halo, idx, adj, stage,
    sx_sem, rx_sem, sz_sem, rz_sem, sg_sem, rg_sem, sp_sem, rp_sem, sy_sem, ry_sem, sh_sem, rh_sem,
):
    nv = vol_ref.shape[1]
    ns = surf_ref.shape[1]
    share = out_ref.shape[0]
    vol = lax.axis_index("vol")
    surf = lax.axis_index("surf")
    x, z = surf // NZ, lax.rem(surf, NZ)
    y, core = vol // 2, lax.rem(vol, 2)
    x_peers = [(vol, lax.rem(x + d, NX) * NZ + z) for d in range(1, NX)]
    z_peers = [(vol, x * NZ + lax.rem(z + d, NZ)) for d in range(1, NZ)]
    y_peers = [(lax.rem(y + d, NY) * 2 + core, surf) for d in range(1, NY)]
    partner = (y * 2 + 1 - core, surf)
    right = (vol, lax.rem(surf + 1, PATCHES))
    left = (vol, lax.rem(surf + PATCHES - 1, PATCHES))

    barrier = pltpu.get_barrier_semaphore()
    peers = z_peers + x_peers + y_peers + [partner, left, right]
    for peer in peers:
        pl.semaphore_signal(barrier, inc=1, device_id=peer, device_id_type=MESH)

    def send(src, dst, send_sem, recv_sem, peer):
        copy = pltpu.make_async_remote_copy(
            src_ref=src, dst_ref=dst, send_sem=send_sem, recv_sem=recv_sem, device_id=peer, device_id_type=MESH
        )
        copy.start()
        return copy

    for axis in range(3):
        for block in range(ns // LANES):
            row = surf_ref[axis : axis + 1, block * LANES : (block + 1) * LANES]
            surf_cols[axis, block * LANES : (block + 1) * LANES, :] = jnp.transpose(
                jnp.broadcast_to(row, (LANES, LANES))
            )

    def weigh(block, carry):
        lanes = pl.ds(pl.multiple_of(block * LANES, LANES), LANES)
        coords = [jnp.broadcast_to(vol_ref[a : a + 1, lanes], (ROWS_W, LANES)) for a in range(3)]

        def chunk(step, sums):
            rows = pl.ds(pl.multiple_of(step * ROWS_W, ROWS_W), ROWS_W)
            delta = [coords[a] - surf_cols[a, rows, :] for a in range(3)]
            dist = delta[0] * delta[0] + delta[1] * delta[1] + delta[2] * delta[2]
            near, far = dist + near_square, dist + far_square
            near = near * near
            top = (near_square * near_square) * far + (far_weight * far_square) * near
            value = top * pl.reciprocal(near * far)
            high, low = split(value)
            w_high[rows, lanes] = high
            w_low[rows, lanes] = low
            return sums + jnp.sum(value.reshape(ROWS_W // 8, 8, LANES), axis=0)

        sums = lax.fori_loop(0, ns // ROWS_W, chunk, jnp.zeros((8, LANES), jnp.float32), unroll=2)
        tot[block // 8, pl.ds(lax.rem(block, 8), 1), :] = jnp.sum(sums, axis=0, keepdims=True)
        return carry

    lax.fori_loop(0, nv // LANES, weigh, 0)

    links = links_ref[...]
    patch = jnp.bitwise_and(jnp.right_shift(links, 10) - surf + (PATCHES + 1), PATCHES - 1)
    valid = links >= 0
    idx[...] = jnp.where(valid, patch * ns + jnp.bitwise_and(links, ns - 1), -1)
    degree = jnp.sum(jnp.where(valid, 1.0, 0.0), axis=0, keepdims=True)
    diagonal = 1.0 / (1.0 + smoothing * degree)

    def count(first, last):
        def lane_block(block, carry):
            lanes = pl.ds(pl.multiple_of(block * LANES, LANES), LANES)
            wanted = [jnp.broadcast_to(idx[k : k + 1, lanes], (ROWS_A, LANES)) for k in range(idx.shape[0])]
            iota = lax.broadcasted_iota(jnp.int32, (ROWS_A, LANES), 0)

            def chunk(step, inner):
                start = pl.multiple_of(step * ROWS_A, ROWS_A)
                node = iota + start
                total = jnp.where(node == wanted[0], 1.0, 0.0)
                for k in range(1, len(wanted)):
                    total = total + jnp.where(node == wanted[k], 1.0, 0.0)
                adj[pl.ds(start, ROWS_A), lanes] = total.astype(jnp.bfloat16)
                return inner

            return lax.fori_loop(0, 3 * ns // ROWS_A, chunk, carry)

        lax.fori_loop(first, last, lane_block, 0)

    pl.semaphore_wait(barrier, len(peers))

    copies = [
        send(tot.at[lax.rem(x + d, NX)], rx.at[d - 1], sx_sem.at[d - 1], rx_sem.at[d - 1], x_peers[d - 1])
        for d in range(1, NX)
    ]
    count(0, 2)
    for copy in copies:
        copy.wait()
    zsend[...] = tot[x] + rx[0] + rx[1] + rx[2]
    order = sorted(range(1, NZ), key=lambda d: -min(d, NZ - d))
    copies = [
        send(zsend, zbuf.at[d - 1], sz_sem.at[d - 1], rz_sem.at[d - 1], z_peers[d - 1]) for d in order
    ]
    count(2, 7)
    for copy in copies:
        copy.wait()
    total = zsend[...]
    for d in range(NZ - 1):
        total = total + zbuf[d]
    inv[x] = 1.0 / total
    copies = [
        send(inv.at[x], inv.at[x], sg_sem.at[d - 1], rg_sem.at[d - 1], x_peers[d - 1]) for d in range(1, NX)
    ]
    count(7, 8)
    for copy in copies:
        copy.wait()

    rows = sens_ref.shape[0]
    for block in range(nv // LANES):
        lanes = slice(block * LANES, (block + 1) * LANES)
        high, low = split(
            sens_ref[:, lanes].astype(jnp.float32) * inv[block // 8, block % 8 : block % 8 + 1, :]
        )
        scaled[:rows, lanes] = high
        scaled[rows:, lanes] = low

    def product(step, carry):
        nodes = pl.ds(pl.multiple_of(step * 256, 256), 256)
        both = lax.dot_general(scaled[...], w_high[nodes, :], NT, preferred_element_type=jnp.float32)
        rest = lax.dot_general(scaled[:rows, :], w_low[nodes, :], NT, preferred_element_type=jnp.float32)
        prod[:, nodes] = both[:rows] + both[rows:] + rest
        return carry

    lax.fori_loop(0, ns // 256, product, 0)

    for d in range(2 * NY):
        rs[d % 2, d // 2] = prod[d * share : (d + 1) * share, :]
    copy = send(rs.at[1 - core], pr, sp_sem, rp_sem, partner)
    copy.wait()
    for d in range(NY):
        ysend[d] = rs[core, d] + pr[d]
    copies = [
        send(ysend.at[lax.rem(y + d, NY)], yr.at[d - 1], sy_sem.at[d - 1], ry_sem.at[d - 1], y_peers[d - 1])
        for d in range(1, NY)
    ]
    for copy in copies:
        copy.wait()
    source = ysend[y] + yr[0] + yr[1] + yr[2]
    cur[0] = source

    for slot in range(3):
        stage[slot] = jnp.zeros(stage.shape[1:], jnp.float32)

    def neighbours(value, part):
        stage[part, :share, :] = value
        high, low = split(stage[part])
        both = jnp.concatenate([high, low], axis=0)
        half = high.shape[0]
        result = jnp.dot(both, adj[part * ns : (part + 1) * ns, :], preferred_element_type=jnp.float32)
        return result[:share] + result[half : half + share]

    for sweep in range(SWEEPS):
        to_right = send(cur.at[sweep], halo.at[sweep, 0], sh_sem.at[sweep, 0], rh_sem.at[sweep, 0], right)
        to_left = send(cur.at[sweep], halo.at[sweep, 1], sh_sem.at[sweep, 1], rh_sem.at[sweep, 1], left)
        total = neighbours(cur[sweep], 1)
        to_right.wait()
        total = total + neighbours(halo[sweep, 0], 0)
        to_left.wait()
        total = total + neighbours(halo[sweep, 1], 2)
        result = (source + smoothing * total) * diagonal
        if sweep < SWEEPS - 1:
            cur[sweep + 1] = result
        else:
            out_ref[...] = result


def per_device(vol_coords, surf_coords, vol_sens, links):
    nv, ns, rows = vol_coords.shape[1], surf_coords.shape[1], vol_sens.shape[0]
    share = rows // (2 * NY)
    f32, bf16 = jnp.float32, jnp.bfloat16
    vmem, dma = pltpu.VMEM, pltpu.SemaphoreType.DMA
    return pl.pallas_call(
        kernel,
        out_shape=jax.ShapeDtypeStruct((share, ns), f32),
        in_specs=[pl.BlockSpec(memory_space=vmem)] * 4,
        out_specs=pl.BlockSpec(memory_space=vmem),
        scratch_shapes=[
            vmem((3, ns, LANES), f32),
            vmem((ns, nv), bf16),
            vmem((ns, nv), bf16),
            vmem((NX, 8, LANES), f32),
            vmem((NX - 1, 8, LANES), f32),
            vmem((8, LANES), f32),
            vmem((NZ - 1, 8, LANES), f32),
            vmem((NX, 8, LANES), f32),
            vmem((2 * rows, nv), bf16),
            vmem((rows, ns), f32),
            vmem((2, NY, share, ns), f32),
            vmem((NY, share, ns), f32),
            vmem((NY, share, ns), f32),
            vmem((NY - 1, share, ns), f32),
            vmem((SWEEPS, share, ns), f32),
            vmem((SWEEPS, 2, share, ns), f32),
            vmem(links.shape, jnp.int32),
            vmem((3 * ns, ns), bf16),
            vmem((3, 16, ns), f32),
            dma((NX - 1,)), dma((NX - 1,)),
            dma((NZ - 1,)), dma((NZ - 1,)),
            dma((NX - 1,)), dma((NX - 1,)),
            dma, dma,
            dma((NY - 1,)), dma((NY - 1,)),
            dma((SWEEPS, 2)), dma((SWEEPS, 2)),
        ],
        compiler_params=pltpu.CompilerParams(
            collective_id=0, has_side_effects=True, vmem_limit_bytes=52 * 2**20
        ),
    )(vol_coords, surf_coords, vol_sens, links)


def solution(mesh):
    return jax.shard_map(
        per_device,
        mesh=mesh,
        in_specs=(P(None, "vol"), P(None, "surf"), P(None, "vol"), P(None, "surf")),
        out_specs=P("vol", "surf"),
        check_vma=False,
    )
```

```python
import functools

import jax
import jax.numpy as jnp
from jax import lax
from jax.experimental import pallas as pl
from jax.experimental.pallas import tpu as pltpu
from jax.sharding import PartitionSpec as P

SWEEPS = 4
NX, NZ, NY = 4, 16, 4
PATCHES = NX * NZ
LANES = 128
MESH = pl.DeviceIdType.MESH

near_square = 0.0016
far_square = 4.0
far_weight = 0.001
smoothing = 2.0

ROWS_W = 64
ROWS_A = 128
NODES = 256
NT = (((1,), (1,)), ((), ()))


def split(value):
    high = value.astype(jnp.bfloat16)
    low = (value - high.astype(jnp.float32)).astype(jnp.bfloat16)
    return high, low


def kernel(
    vol_hbm, surf_hbm, sens_hbm, links_hbm, out_ref, vol_ref, surf_ref, sens_ref, links_ref,
    surf_cols, w_high, w_low, tot, rx, zsend, zbuf, inv, scaled, prod, rs, pr, ysend, yr,
    cur, halo, idx, adj, stage,
    sx_sem, rx_sem, sz_sem, rz_sem, sg_sem, rg_sem, sp_sem, rp_sem, sy_sem, ry_sem, sh_sem, rh_sem, in_sem,
):
    nv = vol_ref.shape[1]
    ns = surf_ref.shape[1]
    share = out_ref.shape[0]
    vol = lax.axis_index("vol")
    surf = lax.axis_index("surf")
    x, z = surf // NZ, lax.rem(surf, NZ)
    y, core = vol // 2, lax.rem(vol, 2)
    x_peers = [(vol, lax.rem(x + d, NX) * NZ + z) for d in range(1, NX)]
    z_peers = [(vol, x * NZ + lax.rem(z + d, NZ)) for d in range(1, NZ)]
    y_peers = [(lax.rem(y + d, NY) * 2 + core, surf) for d in range(1, NY)]
    partner = (y * 2 + 1 - core, surf)
    right = (vol, lax.rem(surf + 1, PATCHES))
    left = (vol, lax.rem(surf + PATCHES - 1, PATCHES))

    loads = [
        pltpu.make_async_copy(src, dst, in_sem.at[i])
        for i, (src, dst) in enumerate(
            [(surf_hbm, surf_ref), (vol_hbm, vol_ref), (links_hbm, links_ref), (sens_hbm, sens_ref)]
        )
    ]
    for load in loads:
        load.start()

    barrier = pltpu.get_barrier_semaphore()
    peers = z_peers + x_peers + y_peers + [partner, left, right]
    for peer in peers:
        pl.semaphore_signal(barrier, inc=1, device_id=peer, device_id_type=MESH)

    def send(src, dst, send_sem, recv_sem, peer):
        copy = pltpu.make_async_remote_copy(
            src_ref=src, dst_ref=dst, send_sem=send_sem, recv_sem=recv_sem, device_id=peer, device_id_type=MESH
        )
        copy.start()
        return copy

    loads[0].wait()
    for axis in range(3):
        for block in range(ns // LANES):
            row = surf_ref[axis : axis + 1, block * LANES : (block + 1) * LANES]
            surf_cols[axis, block * LANES : (block + 1) * LANES, :] = jnp.transpose(
                jnp.broadcast_to(row, (LANES, LANES))
            )

    loads[1].wait()
    piece = nv // NX

    def weigh_piece(d):
        owner = lax.rem(x + d, NX)

        def weigh(block, carry):
            source_lanes = pl.ds(pl.multiple_of(owner * piece + block * LANES, LANES), LANES)
            lanes = pl.ds(pl.multiple_of(d * piece + block * LANES, LANES), LANES)
            coords = [jnp.broadcast_to(vol_ref[a : a + 1, source_lanes], (ROWS_W, LANES)) for a in range(3)]

            def chunk(step, sums):
                rows = pl.ds(pl.multiple_of(step * ROWS_W, ROWS_W), ROWS_W)
                delta = [coords[a] - surf_cols[a, rows, :] for a in range(3)]
                dist = delta[0] * delta[0] + delta[1] * delta[1] + delta[2] * delta[2]
                near, far = dist + near_square, dist + far_square
                near = near * near
                top = (near_square * near_square) * far + (far_weight * far_square) * near
                value = top * pl.reciprocal(near * far)
                high, low = split(value)
                w_high[rows, lanes] = high
                w_low[rows, lanes] = low
                return sums + jnp.sum(value.reshape(ROWS_W // 8, 8, LANES), axis=0)

            sums = lax.fori_loop(0, ns // ROWS_W, chunk, jnp.zeros((8, LANES), jnp.float32), unroll=2)
            tot[d, pl.ds(block, 1), :] = jnp.sum(sums, axis=0, keepdims=True)
            return carry

        lax.fori_loop(0, piece // LANES, weigh, 0)

    def send_piece(d):
        return send(tot.at[d], rx.at[d - 1], sx_sem.at[d - 1], rx_sem.at[d - 1], x_peers[d - 1])

    weigh_piece(1)
    weigh_piece(2)
    pl.semaphore_wait(barrier, len(peers))
    copies = [send_piece(1), send_piece(2)]
    weigh_piece(3)
    copies.append(send_piece(3))
    weigh_piece(0)

    for copy in copies:
        copy.wait()
    zsend[...] = tot[0] + rx[0] + rx[1] + rx[2]
    order = sorted(range(1, NZ), key=lambda d: -min(d, NZ - d))
    copies = [
        send(zsend, zbuf.at[d - 1], sz_sem.at[d - 1], rz_sem.at[d - 1], z_peers[d - 1]) for d in order
    ]

    loads[2].wait()
    links = links_ref[...]
    patch = jnp.bitwise_and(jnp.right_shift(links, 10) - surf + (PATCHES + 1), PATCHES - 1)
    valid = links >= 0
    idx[...] = jnp.where(valid, patch * ns + jnp.bitwise_and(links, ns - 1), -1).astype(jnp.float32)
    degree = jnp.sum(jnp.where(valid, 1.0, 0.0), axis=0, keepdims=True)
    diagonal = 1.0 / (1.0 + smoothing * degree)

    iota = lax.broadcasted_iota(jnp.int32, (ROWS_A, LANES), 0).astype(jnp.float32).astype(jnp.bfloat16)
    one, zero = jnp.bfloat16(1.0), jnp.bfloat16(0.0)

    def lane_block(block, carry):
        lanes = pl.ds(pl.multiple_of(block * LANES, LANES), LANES)
        wanted = idx[:, lanes]

        def chunk(step, inner):
            start = pl.multiple_of(step * ROWS_A, ROWS_A)
            near = (wanted - (step * ROWS_A).astype(jnp.float32)).astype(jnp.bfloat16)
            total = None
            for k in range(idx.shape[0]):
                hit = jnp.where(iota == jnp.broadcast_to(near[k : k + 1, :], (ROWS_A, LANES)), one, zero)
                total = hit if total is None else total + hit
            adj[pl.ds(start, ROWS_A), lanes] = total
            return inner

        return lax.fori_loop(0, 3 * ns // ROWS_A, chunk, carry)

    lax.fori_loop(0, ns // LANES, lane_block, 0)
    loads[3].wait()

    for copy in copies:
        copy.wait()
    total = zsend[...]
    for d in range(NZ - 1):
        total = total + zbuf[d]
    inv[x] = 1.0 / total
    copies = [
        send(inv.at[x], inv.at[x], sg_sem.at[d - 1], rg_sem.at[d - 1], x_peers[d - 1]) for d in range(1, NX)
    ]

    rows = sens_ref.shape[0]

    def scale(d):
        owner = lax.rem(x + d, NX)
        for block in range(piece // LANES):
            source_lanes = pl.ds(pl.multiple_of(owner * piece + block * LANES, LANES), LANES)
            lanes = slice(d * piece + block * LANES, d * piece + (block + 1) * LANES)
            high, low = split(sens_ref[:, source_lanes].astype(jnp.float32) * inv[owner, block : block + 1, :])
            scaled[:rows, lanes] = high
            scaled[rows:, lanes] = low

    def product(nodes, lanes):
        both = lax.dot_general(scaled[:, lanes], w_high[nodes, lanes], NT, preferred_element_type=jnp.float32)
        rest = lax.dot_general(scaled[:rows, lanes], w_low[nodes, lanes], NT, preferred_element_type=jnp.float32)
        return both[:rows] + both[rows:] + rest

    def own_product(step, carry):
        nodes = pl.ds(pl.multiple_of(step * NODES, NODES), NODES)
        prod[step] = product(nodes, slice(0, piece))
        return carry

    scale(0)
    lax.fori_loop(0, ns // NODES, own_product, 0)
    for copy in copies:
        copy.wait()
    for d in range(1, NX):
        scale(d)

    def to_y(block, copy):
        copy.wait()
        for d in range(NY):
            ysend[block, d] = rs[block, core, d] + pr[block, d]
        return [
            send(
                ysend.at[block, lax.rem(y + d, NY)], yr.at[block, d - 1],
                sy_sem.at[block, d - 1], ry_sem.at[block, d - 1], y_peers[d - 1],
            )
            for d in range(1, NY)
        ]

    to_partner, copies = None, []
    for block in range(ns // NODES):
        prod[block] = prod[block] + product(slice(block * NODES, (block + 1) * NODES), slice(piece, nv))
        for d in range(2 * NY):
            rs[block, d % 2, d // 2] = prod[block, d * share : (d + 1) * share, :]
        copy = send(rs.at[block, 1 - core], pr.at[block], sp_sem.at[block], rp_sem.at[block], partner)
        if to_partner is not None:
            copies.append(to_y(block - 1, to_partner))
        to_partner = copy
    copies.append(to_y(ns // NODES - 1, to_partner))
    for block in range(ns // NODES):
        for copy in copies[block]:
            copy.wait()
        cur[0, :, block * NODES : (block + 1) * NODES] = (
            ysend[block, y] + yr[block, 0] + yr[block, 1] + yr[block, 2]
        )
    source = cur[0]

    for slot in range(3):
        stage[slot] = jnp.zeros(stage.shape[1:], jnp.float32)

    def neighbours(value, part):
        stage[part, :share, :] = value
        high, low = split(stage[part])
        both = jnp.concatenate([high, low], axis=0)
        half = high.shape[0]
        result = jnp.dot(both, adj[part * ns : (part + 1) * ns, :], preferred_element_type=jnp.float32)
        return result[:share] + result[half : half + share]

    for sweep in range(SWEEPS):
        to_right = send(cur.at[sweep], halo.at[sweep, 0], sh_sem.at[sweep, 0], rh_sem.at[sweep, 0], right)
        to_left = send(cur.at[sweep], halo.at[sweep, 1], sh_sem.at[sweep, 1], rh_sem.at[sweep, 1], left)
        total = neighbours(cur[sweep], 1)
        to_right.wait()
        total = total + neighbours(halo[sweep, 0], 0)
        to_left.wait()
        total = total + neighbours(halo[sweep, 1], 2)
        result = (source + smoothing * total) * diagonal
        if sweep < SWEEPS - 1:
            cur[sweep + 1] = result
        else:
            out_ref[...] = result


def per_device(vol_coords, surf_coords, vol_sens, links):
    nv, ns, rows = vol_coords.shape[1], surf_coords.shape[1], vol_sens.shape[0]
    share, blocks = rows // (2 * NY), ns // NODES
    f32, bf16 = jnp.float32, jnp.bfloat16
    vmem, dma = pltpu.VMEM, pltpu.SemaphoreType.DMA
    return pl.pallas_call(
        kernel,
        out_shape=jax.ShapeDtypeStruct((share, ns), f32),
        in_specs=[pl.BlockSpec(memory_space=pltpu.HBM)] * 4,
        out_specs=pl.BlockSpec(memory_space=vmem),
        scratch_shapes=[
            vmem(vol_coords.shape, f32),
            vmem(surf_coords.shape, f32),
            vmem(vol_sens.shape, bf16),
            vmem(links.shape, jnp.int32),
            vmem((3, ns, LANES), f32),
            vmem((ns, nv), bf16),
            vmem((ns, nv), bf16),
            vmem((NX, 8, LANES), f32),
            vmem((NX - 1, 8, LANES), f32),
            vmem((8, LANES), f32),
            vmem((NZ - 1, 8, LANES), f32),
            vmem((NX, 8, LANES), f32),
            vmem((2 * rows, nv), bf16),
            vmem((blocks, rows, NODES), f32),
            vmem((blocks, 2, NY, share, NODES), f32),
            vmem((blocks, NY, share, NODES), f32),
            vmem((blocks, NY, share, NODES), f32),
            vmem((blocks, NY - 1, share, NODES), f32),
            vmem((SWEEPS, share, ns), f32),
            vmem((SWEEPS, 2, share, ns), f32),
            vmem(links.shape, f32),
            vmem((3 * ns, ns), bf16),
            vmem((3, 16, ns), f32),
            dma((NX - 1,)), dma((NX - 1,)),
            dma((NZ - 1,)), dma((NZ - 1,)),
            dma((NX - 1,)), dma((NX - 1,)),
            dma((blocks,)), dma((blocks,)),
            dma((blocks, NY - 1)), dma((blocks, NY - 1)),
            dma((SWEEPS, 2)), dma((SWEEPS, 2)),
            dma((4,)),
        ],
        compiler_params=pltpu.CompilerParams(
            collective_id=0, has_side_effects=True, vmem_limit_bytes=67_043_328
        ),
    )(vol_coords, surf_coords, vol_sens, links)


def solution(mesh):
    return jax.shard_map(
        per_device,
        mesh=mesh,
        in_specs=(P(None, "vol"), P(None, "surf"), P(None, "vol"), P(None, "surf")),
        out_specs=P("vol", "surf"),
        check_vma=False,
    )
```

```python
import functools

import jax
import jax.numpy as jnp
from jax import lax
from jax.experimental import pallas as pl
from jax.experimental.pallas import tpu as pltpu
from jax.sharding import PartitionSpec as P

SWEEPS = 4
NX, NZ, NY = 4, 16, 4
PATCHES = NX * NZ
LANES = 128
MESH = pl.DeviceIdType.MESH

near_square = 0.0016
far_square = 4.0
far_weight = 0.001
smoothing = 2.0

ROWS_W = 64
ROWS_A = 128
NODES = 256
NT = (((1,), (1,)), ((), ()))


def split(value):
    high = value.astype(jnp.bfloat16)
    low = (value - high.astype(jnp.float32)).astype(jnp.bfloat16)
    return high, low


def kernel(
    vol_hbm, surf_hbm, sens_hbm, links_hbm, out_ref, vol_ref, surf_ref, sens_ref, links_ref,
    surf_cols, w_high, w_low, tot, rx, zsend, zbuf, inv, scaled, prod, rs, pr, ysend, yr,
    cur, packed, halo, idx, adj, stage,
    sx_sem, rx_sem, sz_sem, rz_sem, sg_sem, rg_sem, sp_sem, rp_sem, sy_sem, ry_sem, sh_sem, rh_sem, in_sem,
):
    nv = vol_ref.shape[1]
    ns = surf_ref.shape[1]
    share = out_ref.shape[0]
    vol = lax.axis_index("vol")
    surf = lax.axis_index("surf")
    x, z = surf // NZ, lax.rem(surf, NZ)
    y, core = vol // 2, lax.rem(vol, 2)
    x_peers = [(vol, lax.rem(x + d, NX) * NZ + z) for d in range(1, NX)]
    z_peers = [(vol, x * NZ + lax.rem(z + d, NZ)) for d in range(1, NZ)]
    y_peers = [(lax.rem(y + d, NY) * 2 + core, surf) for d in range(1, NY)]
    partner = (y * 2 + 1 - core, surf)
    right = (vol, lax.rem(surf + 1, PATCHES))
    left = (vol, lax.rem(surf + PATCHES - 1, PATCHES))

    loads = [
        pltpu.make_async_copy(src, dst, in_sem.at[i])
        for i, (src, dst) in enumerate(
            [(surf_hbm, surf_ref), (vol_hbm, vol_ref), (links_hbm, links_ref), (sens_hbm, sens_ref)]
        )
    ]
    for load in loads:
        load.start()

    barrier = pltpu.get_barrier_semaphore()
    peers = z_peers + x_peers + y_peers + [partner, left, right]
    for peer in peers:
        pl.semaphore_signal(barrier, inc=1, device_id=peer, device_id_type=MESH)

    def send(src, dst, send_sem, recv_sem, peer):
        copy = pltpu.make_async_remote_copy(
            src_ref=src, dst_ref=dst, send_sem=send_sem, recv_sem=recv_sem, device_id=peer, device_id_type=MESH
        )
        copy.start()
        return copy

    loads[0].wait()
    for axis in range(3):
        for block in range(ns // LANES):
            row = surf_ref[axis : axis + 1, block * LANES : (block + 1) * LANES]
            surf_cols[axis, block * LANES : (block + 1) * LANES, :] = jnp.transpose(
                jnp.broadcast_to(row, (LANES, LANES))
            )

    loads[1].wait()
    piece = nv // NX

    def weigh_piece(d):
        owner = lax.rem(x + d, NX)

        def weigh(block, carry):
            source_lanes = pl.ds(pl.multiple_of(owner * piece + block * LANES, LANES), LANES)
            lanes = pl.ds(pl.multiple_of(d * piece + block * LANES, LANES), LANES)
            coords = [jnp.broadcast_to(vol_ref[a : a + 1, source_lanes], (ROWS_W, LANES)) for a in range(3)]

            def chunk(step, sums):
                rows = pl.ds(pl.multiple_of(step * ROWS_W, ROWS_W), ROWS_W)
                delta = [coords[a] - surf_cols[a, rows, :] for a in range(3)]
                dist = delta[0] * delta[0] + delta[1] * delta[1] + delta[2] * delta[2]
                near, far = dist + near_square, dist + far_square
                near = near * near
                top = (near_square * near_square) * far + (far_weight * far_square) * near
                value = top * pl.reciprocal(near * far)
                high, low = split(value)
                w_high[rows, lanes] = high
                w_low[rows, lanes] = low
                return sums + jnp.sum(value.reshape(ROWS_W // 8, 8, LANES), axis=0)

            sums = lax.fori_loop(0, ns // ROWS_W, chunk, jnp.zeros((8, LANES), jnp.float32), unroll=2)
            tot[d, pl.ds(block, 1), :] = jnp.sum(sums, axis=0, keepdims=True)
            return carry

        lax.fori_loop(0, piece // LANES, weigh, 0)

    def send_piece(d):
        return send(tot.at[d], rx.at[d - 1], sx_sem.at[d - 1], rx_sem.at[d - 1], x_peers[d - 1])

    for d in range(1, NX):
        weigh_piece(d)
    pl.semaphore_wait(barrier, len(peers))
    copies = [send_piece(d) for d in range(1, NX)]
    weigh_piece(0)

    for copy in copies:
        copy.wait()
    zsend[...] = tot[0] + rx[0] + rx[1] + rx[2]
    order = sorted(range(1, NZ), key=lambda d: -min(d, NZ - d))
    copies = [
        send(zsend, zbuf.at[d - 1], sz_sem.at[d - 1], rz_sem.at[d - 1], z_peers[d - 1]) for d in order
    ]

    loads[2].wait()
    links = links_ref[...]
    patch = jnp.bitwise_and(jnp.right_shift(links, 10) - surf + (PATCHES + 1), PATCHES - 1)
    valid = links >= 0
    idx[...] = jnp.where(valid, patch * ns + jnp.bitwise_and(links, ns - 1), -1).astype(jnp.float32)
    degree = jnp.sum(jnp.where(valid, 1.0, 0.0), axis=0, keepdims=True)
    diagonal = 1.0 / (1.0 + smoothing * degree)

    iota = lax.broadcasted_iota(jnp.int32, (ROWS_A, LANES), 0).astype(jnp.float32).astype(jnp.bfloat16)
    one, zero = jnp.bfloat16(1.0), jnp.bfloat16(0.0)

    def lane_block(block, carry):
        lanes = pl.ds(pl.multiple_of(block * LANES, LANES), LANES)
        wanted = idx[:, lanes]

        def chunk(step, inner):
            start = pl.multiple_of(step * ROWS_A, ROWS_A)
            near = (wanted - (step * ROWS_A).astype(jnp.float32)).astype(jnp.bfloat16)
            total = None
            for k in range(idx.shape[0]):
                hit = jnp.where(iota == jnp.broadcast_to(near[k : k + 1, :], (ROWS_A, LANES)), one, zero)
                total = hit if total is None else total + hit
            adj[pl.ds(start, ROWS_A), lanes] = total
            return inner

        return lax.fori_loop(0, 3 * ns // ROWS_A, chunk, carry)

    lax.fori_loop(0, ns // LANES, lane_block, 0)
    loads[3].wait()

    for copy in copies:
        copy.wait()
    total = zsend[...]
    for d in range(NZ - 1):
        total = total + zbuf[d]
    inv[x] = 1.0 / total
    copies = [
        send(inv.at[x], inv.at[x], sg_sem.at[d - 1], rg_sem.at[d - 1], x_peers[d - 1]) for d in range(1, NX)
    ]

    rows = sens_ref.shape[0]

    def scale(d):
        owner = lax.rem(x + d, NX)
        for block in range(piece // LANES):
            source_lanes = pl.ds(pl.multiple_of(owner * piece + block * LANES, LANES), LANES)
            lanes = slice(d * piece + block * LANES, d * piece + (block + 1) * LANES)
            high, low = split(sens_ref[:, source_lanes].astype(jnp.float32) * inv[owner, block : block + 1, :])
            scaled[:rows, lanes] = high
            scaled[rows:, lanes] = low

    def product(nodes, lanes):
        both = lax.dot_general(scaled[:, lanes], w_high[nodes, lanes], NT, preferred_element_type=jnp.float32)
        rest = lax.dot_general(scaled[:rows, lanes], w_low[nodes, lanes], NT, preferred_element_type=jnp.float32)
        return both[:rows] + both[rows:] + rest

    def own_product(step, carry):
        nodes = pl.ds(pl.multiple_of(step * NODES, NODES), NODES)
        prod[step] = product(nodes, slice(0, piece))
        return carry

    scale(0)
    lax.fori_loop(0, ns // NODES, own_product, 0)
    for copy in copies:
        copy.wait()
    for d in range(1, NX):
        scale(d)

    def to_y(block, copy):
        copy.wait()
        for d in range(NY):
            ysend[block, d] = rs[block, core, d] + pr[block, d]
        return [
            send(
                ysend.at[block, lax.rem(y + d, NY)], yr.at[block, d - 1],
                sy_sem.at[block, d - 1], ry_sem.at[block, d - 1], y_peers[d - 1],
            )
            for d in range(1, NY)
        ]

    to_partner, copies = None, []
    for block in range(ns // NODES):
        prod[block] = prod[block] + product(slice(block * NODES, (block + 1) * NODES), slice(piece, nv))
        for d in range(2 * NY):
            rs[block, d % 2, d // 2] = prod[block, d * share : (d + 1) * share, :]
        copy = send(rs.at[block, 1 - core], pr.at[block], sp_sem.at[block], rp_sem.at[block], partner)
        if to_partner is not None:
            copies.append(to_y(block - 1, to_partner))
        to_partner = copy
    copies.append(to_y(ns // NODES - 1, to_partner))
    for slot in range(3):
        stage[slot] = jnp.zeros(stage.shape[1:], jnp.float32)

    half = ns // 2
    quarters = [slice(q * NODES, (q + 1) * NODES) for q in range(4)]

    def send_half(sweep, part):
        for q in range(2):
            packed[sweep, part, q * share : (q + 1) * share, :] = stage[1, :share, quarters[2 * part + q]]
        return [
            send(
                packed.at[sweep, part], halo.at[sweep, side, part],
                sh_sem.at[sweep, side, part], rh_sem.at[sweep, side, part], peer,
            )
            for side, peer in enumerate((right, left))
        ]

    def neighbours(slot, nodes, columns):
        high, low = split(stage[slot, :, nodes])
        both = jnp.concatenate([high, low], axis=0)
        rows = slice(slot * ns + nodes.start, slot * ns + nodes.stop)
        result = jnp.dot(both, adj[rows, columns], preferred_element_type=jnp.float32)
        return result[:share] + result[high.shape[0] : high.shape[0] + share]

    halves = [slice(0, half), slice(half, ns)]
    whole = slice(0, ns)
    sent = []
    for part in range(2):
        for block in range(2 * part, 2 * part + 2):
            for copy in copies[block]:
                copy.wait()
            value = ysend[block, y] + yr[block, 0] + yr[block, 1] + yr[block, 2]
            cur[:, quarters[block]] = value
            stage[1, :share, quarters[block]] = value
        sent.append(send_half(0, part))

    for sweep in range(SWEEPS):
        total = neighbours(1, whole, whole)
        arriving, sent = sent, []
        for part in range(2):
            for side in range(2):
                arriving[part][side].wait()
                for q in range(2):
                    stage[2 * side, :share, quarters[2 * part + q]] = halo[
                        sweep, side, part, q * share : (q + 1) * share, :
                    ]
            if part == 0:
                total = total + (neighbours(0, halves[0], whole) + neighbours(2, halves[0], whole))
        for part in range(2):
            nodes = halves[part]
            last = neighbours(0, halves[1], nodes) + neighbours(2, halves[1], nodes)
            result = (cur[:, nodes] + smoothing * (total[:, nodes] + last)) * diagonal[:, nodes]
            if sweep < SWEEPS - 1:
                stage[1, :share, nodes] = result
                sent.append(send_half(sweep + 1, part))
            else:
                out_ref[:, nodes] = result


def per_device(vol_coords, surf_coords, vol_sens, links):
    nv, ns, rows = vol_coords.shape[1], surf_coords.shape[1], vol_sens.shape[0]
    share, blocks = rows // (2 * NY), ns // NODES
    f32, bf16 = jnp.float32, jnp.bfloat16
    vmem, dma = pltpu.VMEM, pltpu.SemaphoreType.DMA
    return pl.pallas_call(
        kernel,
        out_shape=jax.ShapeDtypeStruct((share, ns), f32),
        in_specs=[pl.BlockSpec(memory_space=pltpu.HBM)] * 4,
        out_specs=pl.BlockSpec(memory_space=vmem),
        scratch_shapes=[
            vmem(vol_coords.shape, f32),
            vmem(surf_coords.shape, f32),
            vmem(vol_sens.shape, bf16),
            vmem(links.shape, jnp.int32),
            vmem((3, ns, LANES), f32),
            vmem((ns, nv), bf16),
            vmem((ns, nv), bf16),
            vmem((NX, 8, LANES), f32),
            vmem((NX - 1, 8, LANES), f32),
            vmem((8, LANES), f32),
            vmem((NZ - 1, 8, LANES), f32),
            vmem((NX, 8, LANES), f32),
            vmem((2 * rows, nv), bf16),
            vmem((blocks, rows, NODES), f32),
            vmem((blocks, 2, NY, share, NODES), f32),
            vmem((blocks, NY, share, NODES), f32),
            vmem((blocks, NY, share, NODES), f32),
            vmem((blocks, NY - 1, share, NODES), f32),
            vmem((share, ns), f32),
            vmem((SWEEPS, 2, 2 * share, NODES), f32),
            vmem((SWEEPS, 2, 2, 2 * share, NODES), f32),
            vmem(links.shape, f32),
            vmem((3 * ns, ns), bf16),
            vmem((3, 16, ns), f32),
            dma((NX - 1,)), dma((NX - 1,)),
            dma((NZ - 1,)), dma((NZ - 1,)),
            dma((NX - 1,)), dma((NX - 1,)),
            dma((blocks,)), dma((blocks,)),
            dma((blocks, NY - 1)), dma((blocks, NY - 1)),
            dma((SWEEPS, 2, 2)), dma((SWEEPS, 2, 2)),
            dma((4,)),
        ],
        compiler_params=pltpu.CompilerParams(
            collective_id=0, has_side_effects=True, vmem_limit_bytes=67_043_328
        ),
    )(vol_coords, surf_coords, vol_sens, links)


def solution(mesh):
    return jax.shard_map(
        per_device,
        mesh=mesh,
        in_specs=(P(None, "vol"), P(None, "surf"), P(None, "vol"), P(None, "surf")),
        out_specs=P("vol", "surf"),
        check_vma=False,
    )
```

```python
import functools

import jax
import jax.numpy as jnp
from jax import lax
from jax.experimental import pallas as pl
from jax.experimental.pallas import tpu as pltpu
from jax.sharding import PartitionSpec as P

SWEEPS = 4
NX, NZ, NY = 4, 16, 4
PATCHES = NX * NZ
LANES = 128
MESH = pl.DeviceIdType.MESH

near_square = 0.0016
far_square = 4.0
far_weight = 0.001
smoothing = 2.0

ROWS_W = 64
ROWS_A = 128
NODES = 256
NT = (((1,), (1,)), ((), ()))


def split(value):
    high = value.astype(jnp.bfloat16)
    low = (value - high.astype(jnp.float32)).astype(jnp.bfloat16)
    return high, low


def kernel(
    vol_hbm, surf_hbm, sens_hbm, links_hbm, out_ref, vol_ref, surf_ref, sens_ref, links_ref,
    surf_cols, w_high, w_low, tot, rx, zsend, zbuf, inv, scaled, prod, rs, pr, ysend, yr,
    cur, packed, halo, idx, adj, stage,
    sx_sem, rx_sem, sz_sem, rz_sem, sg_sem, rg_sem, sp_sem, rp_sem, sy_sem, ry_sem, sh_sem, rh_sem, in_sem,
):
    nv = vol_ref.shape[1]
    ns = surf_ref.shape[1]
    share = out_ref.shape[0]
    vol = lax.axis_index("vol")
    surf = lax.axis_index("surf")
    x, z = surf // NZ, lax.rem(surf, NZ)
    y, core = vol // 2, lax.rem(vol, 2)
    x_peers = [(vol, lax.rem(x + d, NX) * NZ + z) for d in range(1, NX)]
    z_peers = [(vol, x * NZ + lax.rem(z + d, NZ)) for d in range(1, NZ)]
    y_peers = [(lax.rem(y + d, NY) * 2 + core, surf) for d in range(1, NY)]
    partner = (y * 2 + 1 - core, surf)
    right = (vol, lax.rem(surf + 1, PATCHES))
    left = (vol, lax.rem(surf + PATCHES - 1, PATCHES))

    loads = [
        pltpu.make_async_copy(src, dst, in_sem.at[i])
        for i, (src, dst) in enumerate(
            [(surf_hbm, surf_ref), (vol_hbm, vol_ref), (links_hbm, links_ref), (sens_hbm, sens_ref)]
        )
    ]
    for load in loads:
        load.start()

    barrier = pltpu.get_barrier_semaphore()
    peers = z_peers + x_peers + y_peers + [partner, left, right]
    for peer in peers:
        pl.semaphore_signal(barrier, inc=1, device_id=peer, device_id_type=MESH)

    def send(src, dst, send_sem, recv_sem, peer):
        copy = pltpu.make_async_remote_copy(
            src_ref=src, dst_ref=dst, send_sem=send_sem, recv_sem=recv_sem, device_id=peer, device_id_type=MESH
        )
        copy.start()
        return copy

    loads[0].wait()
    unit = 1.0 / near_square**0.5
    origin = [surf.astype(jnp.float32), 0.0, 0.0]
    for axis in range(3):
        for block in range(ns // LANES):
            row = (surf_ref[axis : axis + 1, block * LANES : (block + 1) * LANES] - origin[axis]) * unit
            surf_cols[axis, block * LANES : (block + 1) * LANES, :] = jnp.transpose(
                jnp.broadcast_to(row, (LANES, LANES))
            )

    loads[1].wait()
    piece = nv // NX

    def weigh_piece(d):
        owner = lax.rem(x + d, NX)

        def weigh(block, carry):
            source_lanes = pl.ds(pl.multiple_of(owner * piece + block * LANES, LANES), LANES)
            lanes = pl.ds(pl.multiple_of(d * piece + block * LANES, LANES), LANES)
            coords = [
                jnp.broadcast_to((vol_ref[a : a + 1, source_lanes] - origin[a]) * unit, (ROWS_W, LANES))
                for a in range(3)
            ]

            def chunk(step, sums):
                rows = pl.ds(pl.multiple_of(step * ROWS_W, ROWS_W), ROWS_W)
                delta = [coords[a] - surf_cols[a, rows, :] for a in range(3)]
                dist = delta[0] * delta[0] + delta[1] * delta[1] + delta[2] * delta[2]
                near, far = dist + 1.0, dist + far_square / near_square
                near = near * near
                top = far + (far_weight * far_square / near_square) * near
                value = top * pl.reciprocal(near * far)
                high, low = split(value)
                w_high[rows, lanes] = high
                w_low[rows, lanes] = low
                return sums + jnp.sum(value.reshape(ROWS_W // 8, 8, LANES), axis=0)

            sums = lax.fori_loop(0, ns // ROWS_W, chunk, jnp.zeros((8, LANES), jnp.float32), unroll=2)
            tot[d, pl.ds(block, 1), :] = jnp.sum(sums, axis=0, keepdims=True)
            return carry

        lax.fori_loop(0, piece // LANES, weigh, 0)

    def send_piece(d):
        return send(tot.at[d], rx.at[d - 1], sx_sem.at[d - 1], rx_sem.at[d - 1], x_peers[d - 1])

    for d in range(1, NX):
        weigh_piece(d)
    pl.semaphore_wait(barrier, len(peers))
    copies = [send_piece(d) for d in range(1, NX)]
    weigh_piece(0)

    for copy in copies:
        copy.wait()
    zsend[...] = tot[0] + rx[0] + rx[1] + rx[2]
    order = sorted(range(1, NZ), key=lambda d: -min(d, NZ - d))
    copies = [
        send(zsend, zbuf.at[d - 1], sz_sem.at[d - 1], rz_sem.at[d - 1], z_peers[d - 1]) for d in order
    ]

    loads[2].wait()
    links = links_ref[...]
    patch = jnp.bitwise_and(jnp.right_shift(links, 10) - surf + (PATCHES + 1), PATCHES - 1)
    valid = links >= 0
    idx[...] = jnp.where(valid, patch * ns + jnp.bitwise_and(links, ns - 1), -1).astype(jnp.float32)
    degree = jnp.sum(jnp.where(valid, 1.0, 0.0), axis=0, keepdims=True)
    diagonal = 1.0 / (1.0 + smoothing * degree)

    iota = lax.broadcasted_iota(jnp.int32, (ROWS_A, LANES), 0).astype(jnp.float32).astype(jnp.bfloat16)
    one, zero = jnp.bfloat16(1.0), jnp.bfloat16(0.0)

    def lane_block(block, carry):
        lanes = pl.ds(pl.multiple_of(block * LANES, LANES), LANES)
        wanted = idx[:, lanes]

        def chunk(step, inner):
            start = pl.multiple_of(step * ROWS_A, ROWS_A)
            near = (wanted - (step * ROWS_A).astype(jnp.float32)).astype(jnp.bfloat16)
            total = None
            for k in range(idx.shape[0]):
                hit = jnp.where(iota == jnp.broadcast_to(near[k : k + 1, :], (ROWS_A, LANES)), one, zero)
                total = hit if total is None else total + hit
            adj[pl.ds(start, ROWS_A), lanes] = total
            return inner

        return lax.fori_loop(0, 3 * ns // ROWS_A, chunk, carry)

    lax.fori_loop(0, ns // LANES, lane_block, 0)
    loads[3].wait()

    for copy in copies:
        copy.wait()
    total = zsend[...]
    for d in range(NZ - 1):
        total = total + zbuf[d]
    inv[x] = 1.0 / total
    copies = [
        send(inv.at[x], inv.at[x], sg_sem.at[d - 1], rg_sem.at[d - 1], x_peers[d - 1]) for d in range(1, NX)
    ]

    rows = sens_ref.shape[0]

    def scale(d):
        owner = lax.rem(x + d, NX)
        for block in range(piece // LANES):
            source_lanes = pl.ds(pl.multiple_of(owner * piece + block * LANES, LANES), LANES)
            lanes = slice(d * piece + block * LANES, d * piece + (block + 1) * LANES)
            high, low = split(sens_ref[:, source_lanes].astype(jnp.float32) * inv[owner, block : block + 1, :])
            scaled[:rows, lanes] = high
            scaled[rows:, lanes] = low

    def product(nodes, lanes):
        both = lax.dot_general(scaled[:, lanes], w_high[nodes, lanes], NT, preferred_element_type=jnp.float32)
        rest = lax.dot_general(scaled[:rows, lanes], w_low[nodes, lanes], NT, preferred_element_type=jnp.float32)
        return both[:rows] + both[rows:] + rest

    def own_product(step, carry):
        nodes = pl.ds(pl.multiple_of(step * NODES, NODES), NODES)
        prod[step] = product(nodes, slice(0, piece))
        return carry

    scale(0)
    lax.fori_loop(0, ns // NODES, own_product, 0)
    for copy in copies:
        copy.wait()
    for d in range(1, NX):
        scale(d)

    def to_y(block, copy):
        copy.wait()
        for d in range(NY):
            ysend[block, d] = rs[block, core, d] + pr[block, d]
        return [
            send(
                ysend.at[block, lax.rem(y + d, NY)], yr.at[block, d - 1],
                sy_sem.at[block, d - 1], ry_sem.at[block, d - 1], y_peers[d - 1],
            )
            for d in range(1, NY)
        ]

    to_partner, copies = None, []
    for block in range(ns // NODES):
        prod[block] = prod[block] + product(slice(block * NODES, (block + 1) * NODES), slice(piece, nv))
        for d in range(2 * NY):
            rs[block, d % 2, d // 2] = prod[block, d * share : (d + 1) * share, :]
        copy = send(rs.at[block, 1 - core], pr.at[block], sp_sem.at[block], rp_sem.at[block], partner)
        if to_partner is not None:
            copies.append(to_y(block - 1, to_partner))
        to_partner = copy
    copies.append(to_y(ns // NODES - 1, to_partner))
    for slot in range(3):
        stage[slot] = jnp.zeros(stage.shape[1:], jnp.float32)

    half = ns // 2
    quarters = [slice(q * NODES, (q + 1) * NODES) for q in range(4)]

    def send_half(sweep, part):
        for q in range(2):
            packed[sweep, part, q * share : (q + 1) * share, :] = stage[1, :share, quarters[2 * part + q]]
        return [
            send(
                packed.at[sweep, part], halo.at[sweep, side, part],
                sh_sem.at[sweep, side, part], rh_sem.at[sweep, side, part], peer,
            )
            for side, peer in enumerate((right, left))
        ]

    def neighbours(slot, nodes, columns):
        high, low = split(stage[slot, :, nodes])
        both = jnp.concatenate([high, low], axis=0)
        rows = slice(slot * ns + nodes.start, slot * ns + nodes.stop)
        result = jnp.dot(both, adj[rows, columns], preferred_element_type=jnp.float32)
        return result[:share] + result[high.shape[0] : high.shape[0] + share]

    halves = [slice(0, half), slice(half, ns)]
    whole = slice(0, ns)
    sent = []
    for part in range(2):
        for block in range(2 * part, 2 * part + 2):
            for copy in copies[block]:
                copy.wait()
            value = ysend[block, y] + yr[block, 0] + yr[block, 1] + yr[block, 2]
            cur[:, quarters[block]] = value
            stage[1, :share, quarters[block]] = value
        sent.append(send_half(0, part))

    for sweep in range(SWEEPS):
        total = neighbours(1, whole, whole)
        arriving, sent = sent, []
        for part in range(2):
            for side in range(2):
                arriving[part][side].wait()
                for q in range(2):
                    stage[2 * side, :share, quarters[2 * part + q]] = halo[
                        sweep, side, part, q * share : (q + 1) * share, :
                    ]
            if part == 0:
                total = total + (neighbours(0, halves[0], whole) + neighbours(2, halves[0], whole))
        for part in range(2):
            nodes = halves[part]
            last = neighbours(0, halves[1], nodes) + neighbours(2, halves[1], nodes)
            result = (cur[:, nodes] + smoothing * (total[:, nodes] + last)) * diagonal[:, nodes]
            if sweep < SWEEPS - 1:
                stage[1, :share, nodes] = result
                sent.append(send_half(sweep + 1, part))
            else:
                out_ref[:, nodes] = result


def per_device(vol_coords, surf_coords, vol_sens, links):
    nv, ns, rows = vol_coords.shape[1], surf_coords.shape[1], vol_sens.shape[0]
    share, blocks = rows // (2 * NY), ns // NODES
    f32, bf16 = jnp.float32, jnp.bfloat16
    vmem, dma = pltpu.VMEM, pltpu.SemaphoreType.DMA
    return pl.pallas_call(
        kernel,
        out_shape=jax.ShapeDtypeStruct((share, ns), f32),
        in_specs=[pl.BlockSpec(memory_space=pltpu.HBM)] * 4,
        out_specs=pl.BlockSpec(memory_space=vmem),
        scratch_shapes=[
            vmem(vol_coords.shape, f32),
            vmem(surf_coords.shape, f32),
            vmem(vol_sens.shape, bf16),
            vmem(links.shape, jnp.int32),
            vmem((3, ns, LANES), f32),
            vmem((ns, nv), bf16),
            vmem((ns, nv), bf16),
            vmem((NX, 8, LANES), f32),
            vmem((NX - 1, 8, LANES), f32),
            vmem((8, LANES), f32),
            vmem((NZ - 1, 8, LANES), f32),
            vmem((NX, 8, LANES), f32),
            vmem((2 * rows, nv), bf16),
            vmem((blocks, rows, NODES), f32),
            vmem((blocks, 2, NY, share, NODES), f32),
            vmem((blocks, NY, share, NODES), f32),
            vmem((blocks, NY, share, NODES), f32),
            vmem((blocks, NY - 1, share, NODES), f32),
            vmem((share, ns), f32),
            vmem((SWEEPS, 2, 2 * share, NODES), f32),
            vmem((SWEEPS, 2, 2, 2 * share, NODES), f32),
            vmem(links.shape, f32),
            vmem((3 * ns, ns), bf16),
            vmem((3, 16, ns), f32),
            dma((NX - 1,)), dma((NX - 1,)),
            dma((NZ - 1,)), dma((NZ - 1,)),
            dma((NX - 1,)), dma((NX - 1,)),
            dma((blocks,)), dma((blocks,)),
            dma((blocks, NY - 1)), dma((blocks, NY - 1)),
            dma((SWEEPS, 2, 2)), dma((SWEEPS, 2, 2)),
            dma((4,)),
        ],
        compiler_params=pltpu.CompilerParams(
            collective_id=0, has_side_effects=True, vmem_limit_bytes=67_043_328
        ),
    )(vol_coords, surf_coords, vol_sens, links)


def solution(mesh):
    return jax.shard_map(
        per_device,
        mesh=mesh,
        in_specs=(P(None, "vol"), P(None, "surf"), P(None, "vol"), P(None, "surf")),
        out_specs=P("vol", "surf"),
        check_vma=False,
    )
```
